32 devices in a mesh: dp: 16 (over z, y, core), tensor: 2 (over x).
Axes of the slice: x: 2, y: 2, z: 4, core: 2. Of those that a mesh axis runs over, the one named last changes fastest.
Arguments:
- layer_in: bfloat16 [262144, 1024], P('dp', 'tensor'), may hold values from -6 to 6
- out_grad: bfloat16 [262144, 1024], P('dp', 'tensor'), may hold values from -6 to 6
- route_index: int32 [128, 256], P('dp'), may hold values from 0 to 2047, as said below
- segments: int32 [262144], P('dp'), may hold values from 0 to 511, never falling along the last dimension, each value on 1 to 2048 neighbouring positions
- w_project: bfloat16 [3, 1024, 1024], P(None, None, 'tensor'), may hold values from -0.1875 to 0.1875
- w_output: bfloat16 [1024, 1024], P('tensor'), may hold values from -0.75 to 0.75
- w_expand: bfloat16 [1024, 4096], P(None, 'tensor'), may hold values from -0.1875 to 0.1875
- w_reduce: bfloat16 [4096, 1024], P('tensor'), may hold values from -0.125 to 0.125
- gain_first: bfloat16 [1024], replicated, may hold values from 0.5 to 1.5
- gain_second: bfloat16 [1024], replicated, may hold values from 0.5 to 1.5
- w_router: bfloat16 [1024], replicated, may hold values from -0.1875 to 0.1875
Outputs:
- layer_out: bfloat16 [262144, 1024], P('dp', 'tensor')
- input_grad: bfloat16 [262144, 1024], P('dp', 'tensor')
- grad_project: float32 [3, 1024, 1024], P(None, None, 'tensor')
- grad_output: float32 [1024, 1024], P('tensor')
- grad_expand: float32 [1024, 4096], P(None, 'tensor')
- grad_reduce: float32 [4096, 1024], P('tensor')
- grad_gain_first: float32 [1024], P('tensor')
- grad_gain_second: float32 [1024], P('tensor')
- grad_router: float32 [1024], P('tensor')
The draws below stay inside these ranges and needn't reach their ends.
Inputs may be any that keep to these rules, and one draw needn't show every extreme that they name: `route_index`: each row holds 256 distinct positions of one sequence in increasing order. `segments`: document numbers never fall along the tokens; a document has 1 to 2048 tokens and may run past a sequence's end.
All inputs are finite; a program needn't handle non-finite values.
Results may differ from the reference program's by a relative error of at most 0.012.
The reference program's roundings to bfloat16 on the way count: a program that leaves them out, or rounds other values in their place, can miss the bound.
Values may be sent and summed in bfloat16 or wider, within the bound.
No kernel may reach another device: no remote copies, remote signals or barrier semaphores. Data moves between devices by JAX's collectives and lax.ppermute only.
A program may use at most 320 MiB of HBM per device.

```python
import math
import jax
import jax.numpy as jnp
import numpy as np
from jax import lax

D = 1024
HEADS = 16
HEAD_DIM = 64
FF = 4096
SEQ = 2048
CAP = 256
SEQS = 128
TOKENS = 262144
DOCS = 512


def draw_route_index(key, part):
    row_keys = jax.random.split(key, SEQS)

    def one_row(row_key):
        return jnp.sort(jax.random.permutation(row_key, SEQ)[:CAP]).astype(jnp.int32)
    return jax.vmap(one_row)(row_keys)


def level_of(key, shape, pieces, least, largest):
    factor_of, own = 1.0, jax.random.fold_in(key, 6)
    for position, shards_of in pieces:
        draws = jnp.exp(jax.random.uniform(jax.random.fold_in(own, position), (shards_of,), jnp.float32, least / len(pieces), largest / len(pieces)))
        factor_of = factor_of * jnp.repeat(draws, shape[position] // shards_of).reshape([-1 if axis == position else 1 for axis in range(len(shape))])
    return factor_of


def split_up(amount, total, limit, slope):
    weights = [(1 << 20) // math.isqrt(standing ** slope) + 1 for standing in range(2, amount + 1)]
    spare, counts = total - limit - (amount - 1), [1] * (amount - 1)
    while spare > 0:
        candidates = [i for i in range(amount - 1) if counts[i] < limit]
        whole, budget = sum([weights[i] for i in candidates]), spare
        for i in candidates:
            addition = min(limit - counts[i], max(1, budget * weights[i] // whole), spare)
            counts[i] = counts[i] + addition
            spare = spare - addition
    return np.array([limit] + counts)


def ragged(rng, count, total, bound, lean):
    if count == 2:
        one = jax.random.randint(rng, (), max(1, total - bound), min(bound, total - 1) + 1)
        return jnp.stack([one, total - one])
    sizes = jnp.asarray(split_up(count, total, bound, lean), jnp.int32)
    pairs = (count - 1) // 2
    source_of, receiver = sizes[1:1 + 2 * pairs:2], sizes[2:2 + 2 * pairs:2]
    margin = jnp.minimum(source_of - 1, bound - receiver)
    moved = jax.random.randint(jax.random.fold_in(rng, 1), (pairs,), 0, 1 << 20) % (margin + 1)
    sizes = sizes.at[1:1 + 2 * pairs:2].set(source_of - moved).at[2:2 + 2 * pairs:2].set(receiver + moved)
    return sizes[jax.random.permutation(jax.random.fold_in(rng, 2), count)]


def gaussian(rng, shape, scale, bound, pieces=(), held_as=jnp.bfloat16):
    factor_of = level_of(rng, shape, pieces, -0.22, 0.18) if pieces else 1.0
    values = jax.random.normal(rng, shape, jnp.float32) * scale * factor_of
    return jnp.minimum(jnp.maximum(values, -bound), bound).astype(held_as)


def setup_inputs(seed: int = 0) -> dict:
    key_of = jax.random.split(jax.random.key(seed), 12)
    layer_in = gaussian(key_of[0], (TOKENS, D), 1.0, 6.0, ((0, 16), (1, 2)))
    out_grad = gaussian(key_of[1], (TOKENS, D), 1.0, 6.0, ((0, 16), (1, 2)))
    route_index = draw_route_index(jax.random.fold_in(key_of[11], 71), 0)
    segments = jnp.searchsorted(jnp.cumsum(ragged(key_of[3], DOCS, TOKENS, SEQ, 2)), jnp.arange(TOKENS), side="right").astype(jnp.int32)
    w_project = gaussian(key_of[4], (3, D, HEADS * HEAD_DIM), D ** -0.5, 0.1875, ((2, 2),))
    w_output = gaussian(key_of[5], (HEADS * HEAD_DIM, D), (HEADS * HEAD_DIM // 16) ** -0.5, 0.75, ((0, 2),))
    w_expand = gaussian(key_of[6], (D, FF), D ** -0.5, 0.1875, ((1, 2),))
    w_reduce = gaussian(key_of[7], (FF, D), (FF // 2) ** -0.5, 0.125, ((0, 2),))
    gain_first = jnp.clip(1.0 + 0.1 * jax.random.normal(key_of[8], (D,), jnp.float32), 0.5, 1.5).astype(jnp.bfloat16)
    gain_second = jnp.clip(1.0 + 0.1 * jax.random.normal(key_of[9], (D,), jnp.float32), 0.5, 1.5).astype(jnp.bfloat16)
    w_router = gaussian(key_of[10], (D,), D ** -0.5, 0.1875)
    return {"layer_in": layer_in, "out_grad": out_grad, "route_index": route_index, "segments": segments, "w_project": w_project, "w_output": w_output, "w_expand": w_expand, "w_reduce": w_reduce, "gain_first": gain_first, "gain_second": gain_second, "w_router": w_router}


@jax.custom_vjp
def low(v):
    return lax.optimization_barrier(v.astype(jnp.bfloat16)).astype(jnp.float32)

@jax.custom_vjp
def low_back(v):
    return v

def low_keep(v):
    return (low(v), None)

def low_pass(kept, grad):
    return (grad,)

def back_keep(v):
    return (v, None)

def back_low(kept, grad):
    return (low(grad),)
low.defvjp(low_keep, low_pass)
low_back.defvjp(back_keep, back_low)
precise = lax.Precision.HIGHEST

def both_round(values_in):
    return low(low_back(values_in))

def rms_scale(values_in):
    return lax.rsqrt(lax.optimization_barrier(jnp.mean(values_in * values_in, axis=-1, keepdims=True)) + 1e-06)

def branch(rows_in, positions, doc_ids, w_project, w_output, w_expand, w_reduce, gain_first, gain_second, w_router):
    router = jnp.dot(rows_in, w_router, precision=precise)
    normed = low(rows_in * rms_scale(rows_in) * gain_first)
    project = both_round(jnp.einsum('rd,cde->cre', normed, w_project, precision=precise))
    queries = project[0].reshape(CAP, HEADS, HEAD_DIM)
    key_rows = project[1].reshape(CAP, HEADS, HEAD_DIM)
    value_rows = project[2].reshape(CAP, HEADS, HEAD_DIM)
    scores = low_back(jnp.einsum('qhe,khe->hqk', queries, key_rows, precision=precise) * HEAD_DIM ** (-0.5))
    allowed = (positions[None, :] <= positions[:, None]) & (doc_ids[None, :] == doc_ids[:, None])
    scores = jnp.where(allowed[None], scores, -1e+30)
    row_top = lax.optimization_barrier(jnp.max(scores, axis=-1, keepdims=True))
    row_expo = jnp.exp(scores - row_top)
    attend_prob = row_expo / lax.optimization_barrier(jnp.sum(row_expo, axis=-1, keepdims=True))
    attended = jnp.einsum('hqk,khe->qhe', low(attend_prob), value_rows, precision=precise)
    attended = both_round(attended.reshape(CAP, HEADS * HEAD_DIM))
    attn_out = low_back(jnp.dot(attended, w_output, precision=precise))
    hidden = rows_in + attn_out
    normed_two = low(hidden * rms_scale(hidden) * gain_second)
    expand = low_back(jnp.dot(normed_two, w_expand, precision=precise))
    activated = low(jax.nn.gelu(expand, approximate=True))
    mixer_out = low_back(jnp.dot(activated, w_reduce, precision=precise))
    return router[:, None] * (attn_out + mixer_out)

def reference(layer_in, out_grad, route_index, segments, w_project, w_output, w_expand, w_reduce, gain_first, gain_second, w_router):
    weights = tuple((item.astype(jnp.float32) for item in (w_project, w_output, w_expand, w_reduce, gain_first, gain_second, w_router)))
    seq_count = route_index.shape[0]
    in_seq = layer_in.reshape(seq_count, SEQ, D)
    grad_seq = out_grad.reshape(seq_count, SEQ, D)
    doc_seq = segments.reshape(seq_count, SEQ)

    def one_sequence(running, inputs):
        x_rows, d_rows, positions, doc_all = inputs
        rows_in = x_rows[positions].astype(jnp.float32)
        doc_ids = doc_all[positions]
        cot_rows = d_rows[positions].astype(jnp.float32)

        def apply_branch(rows_arg, *params):
            return branch(rows_arg, positions, doc_ids, *params)
        branch_delta, pullback = jax.vjp(apply_branch, rows_in, *weights)
        pulled = pullback(cot_rows)
        new_out = x_rows.at[positions].set((rows_in + branch_delta).astype(jnp.bfloat16))
        new_grad = d_rows.at[positions].set((cot_rows + pulled[0]).astype(jnp.bfloat16))
        running = tuple((acc + item for acc, item in zip(running, pulled[1:])))
        return (running, (new_out, new_grad))
    zero_grads = tuple((jnp.zeros_like(item) for item in weights))
    totals, (out_seq, dx_seq) = lax.scan(one_sequence, zero_grads, (in_seq, grad_seq, route_index, doc_seq))
    return (out_seq.reshape(layer_in.shape), dx_seq.reshape(layer_in.shape), totals[0], totals[1], totals[2], totals[3], totals[4], totals[5], totals[6])
```

```python
from functools import partial

import jax
import jax.numpy as jnp
from jax import lax
from jax.experimental import pallas as pl
from jax.experimental.pallas import tpu as pltpu
from jax.sharding import PartitionSpec as P

HEAD_DIM = 64
F32 = jnp.float32
BF16 = jnp.bfloat16
NT = (((1,), (1,)), ((), ()))
TN = (((0,), (0,)), ((), ()))
NN = (((1,), (0,)), ((), ()))


def dot(a, b, dims=NN, out=F32):
    return lax.dot_general(a, b, dims, preferred_element_type=F32).astype(out)


def params(limit=None):
    return pltpu.CompilerParams(dimension_semantics=("arbitrary",), vmem_limit_bytes=limit)


def gather_body(idx_ref, seg_ref, a_ref, b_ref, rows_ref, cots_ref, doc_ref):
    idx = idx_ref[0]
    length = a_ref.shape[1]
    hit = lax.broadcasted_iota(jnp.int32, (idx.shape[0], length), 1) == idx
    pick = hit.astype(F32).astype(BF16)
    rows_ref[0] = dot(pick, a_ref[0], out=BF16)
    cots_ref[0] = dot(pick, b_ref[0], out=BF16)
    doc_ref[0] = jnp.sum(jnp.where(hit, seg_ref[0], 0), axis=1, keepdims=True)


def gather_rows(layer_in, out_grad, route_index, segments):
    seqs, cap = route_index.shape
    width = layer_in.shape[1]
    length = layer_in.shape[0] // seqs
    big = pl.BlockSpec((1, length, width), lambda i: (i, 0, 0))
    small = pl.BlockSpec((1, cap, width), lambda i: (i, 0, 0))
    column = pl.BlockSpec((1, cap, 1), lambda i: (i, 0, 0))
    return pl.pallas_call(
        gather_body,
        grid=(seqs,),
        in_specs=[column, pl.BlockSpec((1, 1, length), lambda i: (i, 0, 0)), big, big],
        out_specs=[small, small, column],
        out_shape=[
            jax.ShapeDtypeStruct((seqs, cap, width), BF16),
            jax.ShapeDtypeStruct((seqs, cap, width), BF16),
            jax.ShapeDtypeStruct((seqs, cap, 1), jnp.int32),
        ],
        compiler_params=params(),
        name="gather_rows",
    )(
        route_index[:, :, None],
        segments.reshape(seqs, 1, length),
        layer_in.reshape(seqs, length, width),
        out_grad.reshape(seqs, length, width),
    )


def scatter_body(idx_ref, new_ref, a_ref, out_ref):
    idx = idx_ref[0]
    length = a_ref.shape[1]
    hit = lax.broadcasted_iota(jnp.int32, (length, idx.shape[1]), 0) == idx
    place = hit.astype(F32)
    routed = jnp.max(place, axis=1, keepdims=True) > 0.5
    moved = dot(place.astype(BF16), new_ref[0])
    out_ref[0] = jnp.where(routed, moved, a_ref[0].astype(F32)).astype(BF16)


def scatter_rows(base, rows, route_index):
    seqs, cap = route_index.shape
    width = base.shape[1]
    length = base.shape[0] // seqs
    big = pl.BlockSpec((1, length, width), lambda i: (i, 0, 0))
    out = pl.pallas_call(
        scatter_body,
        grid=(seqs,),
        in_specs=[
            pl.BlockSpec((1, 1, cap), lambda i: (i, 0, 0)),
            pl.BlockSpec((1, cap, width), lambda i: (i, 0, 0)),
            big,
        ],
        out_specs=big,
        out_shape=jax.ShapeDtypeStruct((seqs, length, width), BF16),
        compiler_params=params(),
        name="scatter_rows",
    )(route_index[:, None, :], rows, base.reshape(seqs, length, width))
    return out.reshape(base.shape)


def probs_of(query, key, allowed):
    scores = dot(query, key, NT) * HEAD_DIM ** (-0.5)
    scores = jnp.where(allowed, scores, -1e30)
    expo = jnp.exp(scores - jnp.max(scores, axis=1, keepdims=True))
    return expo / jnp.sum(expo, axis=1, keepdims=True)


def allowed_of(pos_c, pos_r, doc_c, doc_r):
    return (pos_r[0] <= pos_c[0]) & (doc_r[0] == doc_c[0])


def attend_body(pos_c, pos_r, doc_c, doc_r, qkv_ref, out_ref):
    allowed = allowed_of(pos_c, pos_r, doc_c, doc_r)
    for head in range(qkv_ref.shape[2] // HEAD_DIM):
        cols = slice(head * HEAD_DIM, (head + 1) * HEAD_DIM)
        probs = probs_of(qkv_ref[0, :, cols], qkv_ref[1, :, cols], allowed)
        out_ref[:, cols] = dot(probs.astype(BF16), qkv_ref[2, :, cols], out=BF16)


def attend_back_body(pos_c, pos_r, doc_c, doc_r, qkv_ref, grad_ref, out_ref):
    allowed = allowed_of(pos_c, pos_r, doc_c, doc_r)
    scale = HEAD_DIM ** (-0.5)
    for head in range(qkv_ref.shape[2] // HEAD_DIM):
        cols = slice(head * HEAD_DIM, (head + 1) * HEAD_DIM)
        query, key, value = (qkv_ref[c, :, cols] for c in range(3))
        grad = grad_ref[:, cols]
        probs = probs_of(query, key, allowed)
        prob_grad = dot(grad, value, NT)
        row_dot = jnp.sum(probs * prob_grad, axis=1, keepdims=True)
        score_grad = (probs * (prob_grad - row_dot)).astype(BF16)
        out_ref[0, :, cols] = (dot(score_grad, key) * scale).astype(BF16)
        out_ref[1, :, cols] = (dot(score_grad, query, TN) * scale).astype(BF16)
        out_ref[2, :, cols] = dot(probs.astype(BF16), grad, TN, BF16)


def attention(body, masks, cap, qkv, *more):
    width = qkv.shape[2]
    seqs = qkv.shape[1] // cap
    column = pl.BlockSpec((1, cap, 1), lambda i: (i, 0, 0))
    line = pl.BlockSpec((1, 1, cap), lambda i: (i, 0, 0))
    three = pl.BlockSpec((3, cap, width), lambda i: (0, i, 0))
    one = pl.BlockSpec((cap, width), lambda i: (i, 0))
    back = bool(more)
    return pl.pallas_call(
        body,
        grid=(seqs,),
        in_specs=[column, line, column, line, three] + [one] * len(more),
        out_specs=three if back else one,
        out_shape=jax.ShapeDtypeStruct(qkv.shape if back else qkv.shape[1:], BF16),
        compiler_params=params(),
        name="attend_back" if back else "attend",
    )(*masks, qkv, *more)


def gelu_parts(v):
    c = 0.7978845608028654
    th = jnp.tanh(c * (v + 0.044715 * (v * v * v)))
    half = 0.5 * (1.0 + th)
    slope = half + 0.5 * v * (1.0 - th * th) * (c * (1.0 + 3 * 0.044715 * (v * v)))
    return v * half, slope


def shards(
    sizes,
    layer_in,
    out_grad,
    route_index,
    segments,
    w_project,
    w_output,
    w_expand,
    w_reduce,
    gain_first,
    gain_second,
    w_router,
):
    copies, parts = sizes
    seq_local, cap = route_index.shape
    width = layer_in.shape[1]
    full = gain_first.shape[0]
    own_seqs = seq_local // parts
    own_rows = own_seqs * cap
    here = lax.axis_index("tensor")
    place = lax.axis_index("dp")
    core = place & 1

    def shift(value, step):
        return lax.ppermute(value, "tensor", [(s, (s + step) % parts) for s in range(parts)])

    def flip(value, bit):
        return lax.ppermute(value, "dp", [(s, s ^ bit) for s in range(copies)])

    def ordered(pieces):
        stacked = jnp.stack(pieces)
        if parts == 2:
            return [
                jnp.where(here == 0, pieces[0], pieces[1]),
                jnp.where(here == 0, pieces[1], pieces[0]),
            ]
        return [
            lax.dynamic_index_in_dim(stacked, (here - s) % parts, keepdims=False)
            for s in range(parts)
        ]

    def group_at(value, index):
        return lax.dynamic_index_in_dim(value, index % parts, keepdims=False)

    def to_rows(local):
        grouped = local.reshape(parts, own_rows, width)
        pieces = [group_at(grouped, here)]
        for k in range(1, parts):
            pieces.append(shift(group_at(grouped, here + k), k))
        return jnp.concatenate(ordered(pieces), axis=1)

    def to_features(value):
        blocks = value.reshape(own_rows, parts, width).transpose(1, 0, 2)
        pieces = [group_at(blocks, here)]
        for k in range(1, parts):
            pieces.append(shift(group_at(blocks, here + k), k))
        return jnp.concatenate(ordered(pieces), axis=0).reshape(seq_local, cap, width)

    def far(weight, k, axis):
        half = weight.shape[axis] // 2
        mine = lax.dynamic_slice_in_dim(weight, core * half, half, axis)
        mine = shift(mine, -k)
        other = flip(mine, 1)
        return jnp.where(
            core == 0,
            jnp.concatenate([mine, other], axis),
            jnp.concatenate([other, mine], axis),
        )

    def every(weight, axis):
        return [weight] + [far(weight, k, axis) for k in range(1, parts)]

    rows_local, cot_local, docs = gather_rows(layer_in, out_grad, route_index, segments)
    rows_in = to_rows(rows_local)
    project_all = every(w_project, 1)
    output_all = every(w_output, 0)
    cot_in = to_rows(cot_local)
    expand_all = every(w_expand, 0)
    reduce_all = every(w_reduce, 0)
    rows = rows_in.astype(F32)
    cot = cot_in.astype(F32)
    positions = group_at(route_index.reshape(parts, own_seqs, cap), here)
    docs = group_at(docs.reshape(parts, own_seqs, cap), here)
    masks = (positions[:, :, None], positions[:, None, :], docs[:, :, None], docs[:, None, :])
    gain_one = gain_first.astype(F32)
    gain_two = gain_second.astype(F32)
    router_row = w_router.astype(F32)

    router = jnp.sum(rows * router_row, axis=1, keepdims=True)
    scale_first = lax.rsqrt(jnp.mean(rows * rows, axis=1, keepdims=True) + 1e-06)
    normed = (rows * scale_first * gain_one).astype(BF16)
    qkv_all = [
        jnp.einsum("rd,cde->cre", normed, w, preferred_element_type=F32).astype(BF16)
        for w in project_all
    ]
    attended_all = [attention(attend_body, masks, cap, qkv) for qkv in qkv_all]
    attn_out = sum(dot(a, w) for a, w in zip(attended_all, output_all))
    hidden = rows + attn_out
    scale_second = lax.rsqrt(jnp.mean(hidden * hidden, axis=1, keepdims=True) + 1e-06)
    normed_two = (hidden * scale_second * gain_two).astype(BF16)
    mixer_grad = (router * cot).astype(BF16)
    activated_all = []
    slope_all = []
    for w in expand_all:
        act, slope = gelu_parts(dot(normed_two, w))
        activated_all.append(act.astype(BF16))
        slope_all.append(slope.astype(BF16))
    back_all = [
        (dot(mixer_grad, w, NT) * slope.astype(F32)).astype(BF16)
        for w, slope in zip(reduce_all, slope_all)
    ]
    reduce_grads = [dot(a, mixer_grad, TN, BF16) for a in activated_all]
    expand_grads = [dot(normed_two, g, TN, BF16) for g in back_all]

    def reduce_over(grads):
        step = grads[0].shape[0] // copies
        rest = grads[0].shape[1:]

        def add(a, b):
            return (a.astype(F32) + b.astype(F32)).astype(BF16)

        kept = []
        for grad in grads:
            blocks = grad.reshape(copies // 2, 2, step, *rest)
            mine = lax.dynamic_index_in_dim(blocks, core, 1, keepdims=False)
            other = lax.dynamic_index_in_dim(blocks, 1 - core, 1, keepdims=False)
            kept.append(add(mine, flip(other, 1)))
        total = kept[0]
        for k in range(1, parts):
            total = add(total, shift(kept[k], k))
        value = total
        bit = 2
        while bit < copies:
            value = value.reshape((value.shape[0] // 2, 2, step) + tuple(rest))
            mine = lax.dynamic_index_in_dim(value, (place // bit) & 1, 1, keepdims=False)
            other = lax.dynamic_index_in_dim(value, 1 - ((place // bit) & 1), 1, keepdims=False)
            value = add(mine, flip(other, bit))
            bit *= 2
        return value.reshape((step,) + tuple(rest))

    def collect(pieces):
        gathered = lax.all_gather(tuple(pieces), "dp", axis=0, tiled=True)
        return [g.astype(F32) for g in gathered]

    grad_reduce, grad_expand = collect([reduce_over(reduce_grads), reduce_over(expand_grads)])

    mixer_out = sum(dot(a, w) for a, w in zip(activated_all, reduce_all))
    branch = attn_out + mixer_out
    layer_rows = (rows + router * branch).astype(BF16)
    router_grad = jnp.sum(cot * branch, axis=1, keepdims=True)
    layer_out = scatter_rows(layer_in, to_features(layer_rows), route_index)

    two_grad = sum(dot(g, w, NT) for g, w in zip(back_all, expand_all))
    hidden_hat = hidden * scale_second
    weighted_two = two_grad * gain_two
    gain_two_part = jnp.sum(two_grad * hidden_hat, axis=0)
    stat_two = jnp.mean(weighted_two * hidden_hat, axis=1, keepdims=True)
    hidden_grad = scale_second * (weighted_two - hidden_hat * stat_two)
    branch_grad = (router * cot + hidden_grad).astype(BF16)
    output_grads = [dot(a, branch_grad, TN, BF16) for a in attended_all]
    back_heads = [dot(branch_grad, w, NT, BF16) for w in output_all]
    project_back = [
        attention(attend_back_body, masks, cap, qkv, g) for qkv, g in zip(qkv_all, back_heads)
    ]
    project_grads = [
        jnp.einsum("rd,cre->cde", normed, g, preferred_element_type=F32)
        .astype(BF16)
        .reshape(3 * full, -1)
        for g in project_back
    ]
    normed_grad = sum(
        dot(g[c], w[c], NT) for g, w in zip(project_back, project_all) for c in range(3)
    )
    rows_hat = rows * scale_first
    weighted_one = normed_grad * gain_one
    gain_one_part = jnp.sum(normed_grad * rows_hat, axis=0)
    stat_one = jnp.mean(weighted_one * rows_hat, axis=1, keepdims=True)
    first_grad = scale_first * (weighted_one - rows_hat * stat_one)
    rows_grad = cot + hidden_grad + first_grad + router_grad * router_row
    router_part = jnp.sum(router_grad * rows, axis=0)
    input_grad = scatter_rows(out_grad, to_features(rows_grad.astype(BF16)), route_index)

    project_sum, output_sum = collect([reduce_over(project_grads), reduce_over(output_grads)])
    grad_project = project_sum.reshape(3, full, -1)
    small = lax.psum(jnp.stack([gain_one_part, gain_two_part, router_part]), ("dp", "tensor"))
    small = lax.dynamic_slice_in_dim(small, here * width, width, 1)
    return (
        layer_out,
        input_grad,
        grad_project,
        output_sum,
        grad_expand,
        grad_reduce,
        small[0],
        small[1],
        small[2],
    )


def solution(mesh):
    return jax.shard_map(
        partial(shards, (mesh.shape["dp"], mesh.shape["tensor"])),
        mesh=mesh,
        in_specs=(
            P("dp", "tensor"),
            P("dp", "tensor"),
            P("dp", None),
            P("dp"),
            P(None, None, "tensor"),
            P("tensor", None),
            P(None, "tensor"),
            P("tensor", None),
            P(),
            P(),
            P(),
        ),
        out_specs=(
            P("dp", "tensor"),
            P("dp", "tensor"),
            P(None, None, "tensor"),
            P("tensor", None),
            P(None, "tensor"),
            P("tensor", None),
            P("tensor"),
            P("tensor"),
            P("tensor"),
        ),
        check_vma=False,
    )
```

```python
from functools import partial

import jax
import jax.numpy as jnp
from jax import lax
from jax.experimental import pallas as pl
from jax.experimental.pallas import tpu as pltpu
from jax.sharding import PartitionSpec as P


HEAD_DIM = 64
F32 = jnp.float32
BF16 = jnp.bfloat16
NT = (((1,), (1,)), ((), ()))
TN = (((0,), (0,)), ((), ()))
NN = (((1,), (0,)), ((), ()))


def dot(a, b, dims=NN, out=F32):
    return lax.dot_general(a, b, dims, preferred_element_type=F32).astype(out)


hold = lax.optimization_barrier


def params(limit=None):
    return pltpu.CompilerParams(dimension_semantics=("arbitrary",), vmem_limit_bytes=limit)


def gather_body(idx_ref, a_ref, *refs):
    idx = idx_ref[0]
    length = a_ref.shape[1]
    hit = lax.broadcasted_iota(jnp.int32, (idx.shape[0], length), 1) == idx
    refs[-1][0] = dot(hit.astype(F32).astype(BF16), a_ref[0], out=BF16)
    if len(refs) > 1:
        seg_ref, doc_ref, _ = refs
        doc_ref[0] = jnp.sum(jnp.where(hit, seg_ref[0], 0), axis=1, keepdims=True)


def gather_rows(source, route_index, segments=None):
    seqs, cap = route_index.shape
    width = source.shape[1]
    length = source.shape[0] // seqs
    column = pl.BlockSpec((1, cap, 1), lambda i: (i, 0, 0))
    in_specs = [column, pl.BlockSpec((1, length, width), lambda i: (i, 0, 0))]
    args = [route_index[:, :, None], source.reshape(seqs, length, width)]
    out_specs = [pl.BlockSpec((1, cap, width), lambda i: (i, 0, 0))]
    out_shape = [jax.ShapeDtypeStruct((seqs, cap, width), BF16)]
    if segments is not None:
        in_specs.append(pl.BlockSpec((1, 1, length), lambda i: (i, 0, 0)))
        args.append(segments.reshape(seqs, 1, length))
        out_specs.insert(0, column)
        out_shape.insert(0, jax.ShapeDtypeStruct((seqs, cap, 1), jnp.int32))
    return pl.pallas_call(
        gather_body,
        grid=(seqs,),
        in_specs=in_specs,
        out_specs=out_specs,
        out_shape=out_shape,
        compiler_params=params(),
        name="gather_rows",
    )(*args)


def scatter_body(idx_ref, new_ref, a_ref, out_ref):
    idx = idx_ref[0]
    length = a_ref.shape[1]
    hit = lax.broadcasted_iota(jnp.int32, (length, idx.shape[1]), 0) == idx
    place = hit.astype(F32)
    routed = jnp.max(place, axis=1, keepdims=True) > 0.5
    moved = dot(place.astype(BF16), new_ref[0])
    out_ref[0] = jnp.where(routed, moved, a_ref[0].astype(F32)).astype(BF16)


def scatter_rows(base, rows, route_index):
    seqs, cap = route_index.shape
    width = base.shape[1]
    length = base.shape[0] // seqs
    big = pl.BlockSpec((1, length, width), lambda i: (i, 0, 0))
    out = pl.pallas_call(
        scatter_body,
        grid=(seqs,),
        in_specs=[
            pl.BlockSpec((1, 1, cap), lambda i: (i, 0, 0)),
            pl.BlockSpec((1, cap, width), lambda i: (i, 0, 0)),
            big,
        ],
        out_specs=big,
        out_shape=jax.ShapeDtypeStruct((seqs, length, width), BF16),
        compiler_params=params(),
        name="scatter_rows",
    )(route_index[:, None, :], rows, base.reshape(seqs, length, width))
    return out.reshape(base.shape)


def probs_of(query, key, allowed):
    scores = dot(key, query * HEAD_DIM ** (-0.5), NT)
    scores = jnp.where(allowed, scores, -1e30)
    expo = jnp.exp(scores - jnp.max(scores, axis=0, keepdims=True))
    return expo * (1.0 / jnp.sum(expo, axis=0, keepdims=True))


def allowed_of(pos_c, pos_r, doc_c, doc_r):
    return (pos_c[0] <= pos_r[0]) & (doc_r[0] == doc_c[0])


def head_groups(width):
    heads = range(width // HEAD_DIM)
    return [heads[i : i + 2] for i in range(0, len(heads), 2)]


def columns(head, count=1):
    return slice(head * HEAD_DIM, (head + count) * HEAD_DIM)


def attend_body(pos_c, pos_r, doc_c, doc_r, qkv_ref, out_ref):
    allowed = allowed_of(pos_c, pos_r, doc_c, doc_r)
    for group in head_groups(qkv_ref.shape[2]):
        turned = []
        for head in group:
            cols = columns(head)
            probs = probs_of(qkv_ref[0, :, cols], qkv_ref[1, :, cols], allowed)
            turned.append(dot(qkv_ref[2, :, cols], probs.astype(BF16), TN))
        out_ref[:, columns(group[0], len(group))] = jnp.concatenate(turned, 0).T.astype(BF16)


def attend_back_body(pos_c, pos_r, doc_c, doc_r, qkv_ref, grad_ref, out_ref):
    allowed = allowed_of(pos_c, pos_r, doc_c, doc_r)
    scale = HEAD_DIM ** (-0.5)
    for group in head_groups(qkv_ref.shape[2]):
        turned = []
        for head in group:
            cols = columns(head)
            query, key, value = (qkv_ref[c, :, cols] for c in range(3))
            grad = grad_ref[:, cols]
            probs = probs_of(query, key, allowed)
            prob_grad = dot(value, grad, NT)
            row_dot = jnp.sum(probs * prob_grad, axis=0, keepdims=True)
            score_grad = (probs * (prob_grad - row_dot)).astype(BF16)
            turned.append(dot(key, score_grad, TN))
            out_ref[1, :, cols] = (dot(score_grad, query) * scale).astype(BF16)
            out_ref[2, :, cols] = dot(probs.astype(BF16), grad, out=BF16)
        both = jnp.concatenate(turned, 0).T * scale
        out_ref[0, :, columns(group[0], len(group))] = both.astype(BF16)


def attention(body, masks, cap, qkv, *more):
    width = qkv.shape[2]
    seqs = qkv.shape[1] // cap
    column = pl.BlockSpec((1, cap, 1), lambda i: (i, 0, 0))
    line = pl.BlockSpec((1, 1, cap), lambda i: (i, 0, 0))
    three = pl.BlockSpec((3, cap, width), lambda i: (0, i, 0))
    one = pl.BlockSpec((cap, width), lambda i: (i, 0))
    back = bool(more)
    return pl.pallas_call(
        body,
        grid=(seqs,),
        in_specs=[column, line, column, line, three] + [one] * len(more),
        out_specs=three if back else one,
        out_shape=jax.ShapeDtypeStruct(qkv.shape if back else qkv.shape[1:], BF16),
        compiler_params=params(),
        name="attend_back" if back else "attend",
    )(*masks, qkv, *more)


def gelu_parts(v):
    c = 0.7978845608028654
    th = jnp.tanh(c * (v + 0.044715 * (v * v * v)))
    half = 0.5 * (1.0 + th)
    slope = half + 0.5 * v * (1.0 - th * th) * (c * (1.0 + 3 * 0.044715 * (v * v)))
    return v * half, slope


def shards(
    sizes,
    layer_in,
    out_grad,
    route_index,
    segments,
    w_project,
    w_output,
    w_expand,
    w_reduce,
    gain_first,
    gain_second,
    w_router,
):
    copies, parts = sizes
    seq_local, cap = route_index.shape
    width = layer_in.shape[1]
    full = gain_first.shape[0]
    own_seqs = seq_local // parts
    own_rows = own_seqs * cap
    here = lax.axis_index("tensor")
    place = lax.axis_index("dp")
    core = place & 1

    def shift_plain(value, step):
        return lax.ppermute(value, "tensor", [(s, (s + step) % parts) for s in range(parts)])

    def flip_plain(value, bit):
        return lax.ppermute(value, "dp", [(s, s ^ bit) for s in range(copies)])

    def ordered(pieces):
        stacked = jnp.stack(pieces)
        if parts == 2:
            return [
                jnp.where(here == 0, pieces[0], pieces[1]),
                jnp.where(here == 0, pieces[1], pieces[0]),
            ]
        return [
            lax.dynamic_index_in_dim(stacked, (here - s) % parts, keepdims=False)
            for s in range(parts)
        ]

    def group_at(value, index):
        return lax.dynamic_index_in_dim(value, index % parts, keepdims=False)

    def to_rows(local):
        grouped = local.reshape(parts, own_rows, width)
        pieces = [group_at(grouped, here)]
        for k in range(1, parts):
            pieces.append(shift_plain(group_at(grouped, here + k), k))
        return jnp.concatenate(ordered(pieces), axis=1)

    def to_features(value):
        blocks = value.reshape(own_rows, parts, width).transpose(1, 0, 2)
        pieces = [group_at(blocks, here)]
        for k in range(1, parts):
            pieces.append(shift_plain(group_at(blocks, here + k), k))
        return jnp.concatenate(ordered(pieces), axis=0).reshape(seq_local, cap, width)

    def far(weight, k, axis):
        half = weight.shape[axis] // 2
        mine = lax.dynamic_slice_in_dim(weight, core * half, half, axis)
        mine = shift_plain(mine, -k)
        other = flip_plain(mine, 1)
        return jnp.where(
            core == 0,
            jnp.concatenate([mine, other], axis),
            jnp.concatenate([other, mine], axis),
        )

    def spread(weight, k):
        step = weight.shape[0] // copies
        return shift_plain(lax.dynamic_slice_in_dim(weight, place * step, step, 0), -k)

    slices = [(spread(w_expand, k), spread(w_reduce, k)) for k in range(1, parts)]
    docs, rows_local = gather_rows(layer_in, route_index, segments)
    rows_local, slices = hold((rows_local, slices))
    gathered = lax.all_gather(slices, "dp", axis=0, tiled=True)
    expand_all = [w_expand] + [pair[0] for pair in gathered]
    reduce_all = [w_reduce] + [pair[1] for pair in gathered]
    rows_in = to_rows(rows_local)
    (cot_local,) = gather_rows(out_grad, route_index)
    rows_in, cot_local, w_project_late, w_output_late = hold(
        (rows_in, cot_local, w_project, w_output)
    )
    project_far = [far(w_project_late, k, 1) for k in range(1, parts)]
    output_far = [far(w_output_late, k, 0) for k in range(1, parts)]
    cot_local, project_far = hold((cot_local, project_far))
    cot_in = to_rows(cot_local)
    project_all = [w_project] + project_far
    output_all = [w_output] + output_far
    rows = rows_in.astype(F32)
    cot = cot_in.astype(F32)
    positions = group_at(route_index.reshape(parts, own_seqs, cap), here)
    docs = group_at(docs.reshape(parts, own_seqs, cap), here)
    masks = (positions[:, :, None], positions[:, None, :], docs[:, :, None], docs[:, None, :])
    gain_one = gain_first.astype(F32)
    gain_two = gain_second.astype(F32)
    router_row = w_router.astype(F32)

    router = jnp.sum(rows * router_row, axis=1, keepdims=True)
    scale_first = lax.rsqrt(jnp.mean(rows * rows, axis=1, keepdims=True) + 1e-06)
    normed = (rows * scale_first * gain_one).astype(BF16)

    def heads_of(w):
        qkv = jnp.einsum("rd,cde->cre", normed, w, preferred_element_type=F32).astype(BF16)
        return qkv, attention(attend_body, masks, cap, qkv)

    heads_all = [heads_of(w_project)]
    heads_all += [heads_of(w) for w in project_far]
    qkv_all = [pair[0] for pair in heads_all]
    attended_all = [pair[1] for pair in heads_all]
    attn_out = sum(dot(a, w) for a, w in zip(attended_all, output_all))
    hidden = rows + attn_out
    scale_second = lax.rsqrt(jnp.mean(hidden * hidden, axis=1, keepdims=True) + 1e-06)
    normed_two = (hidden * scale_second * gain_two).astype(BF16)
    mixer_grad = (router * cot).astype(BF16)
    activated_all = []
    slope_all = []
    for w in expand_all:
        act, slope = gelu_parts(dot(normed_two, w))
        activated_all.append(act.astype(BF16))
        slope_all.append(slope.astype(BF16))

    def add(a, b):
        return (a.astype(F32) + b.astype(F32)).astype(BF16)

    def blocks_of(grads):
        return [g.reshape((copies, g.shape[0] // copies) + g.shape[1:]) for g in grads]

    def send(values, bit):
        lead = values[0].shape[0] // 2
        pairs = [v.reshape((lead, 2) + v.shape[1:]) for v in values]
        index = (place // bit) & 1
        kept = [lax.dynamic_index_in_dim(v, index, 1, keepdims=False) for v in pairs]
        away = [lax.dynamic_index_in_dim(v, 1 - index, 1, keepdims=False) for v in pairs]
        return kept, [flip_plain(v, bit) for v in away]

    def merge(sent):
        return [add(a, b) for a, b in zip(*sent)]

    def cross(values):
        return values[:1], [shift_plain(values[k], k) for k in range(1, parts)]

    def merge_cross(sent):
        total = sent[0][0]
        for other in sent[1]:
            total = add(total, other)
        return [total]

    def finish(values, bit):
        while bit < copies:
            values = merge(send(values, bit))
            bit *= 2
        return values[0].reshape(values[0].shape[1:])

    reduce_grads = [dot(a, mixer_grad, TN, BF16) for a in activated_all]
    reduce_grads, mixer_grad, slope_all = hold((reduce_grads, mixer_grad, slope_all))
    sent_r = send(blocks_of(reduce_grads), 1)
    back_all = [
        (dot(mixer_grad, w, NT) * slope.astype(F32)).astype(BF16)
        for w, slope in zip(reduce_all, slope_all)
    ]
    back_all, part_r = hold((back_all, merge(sent_r)))
    sent_r = cross(part_r)
    expand_grads = [dot(normed_two, g, TN, BF16) for g in back_all]
    expand_grads, back_all, activated_all = hold((expand_grads, back_all, activated_all))
    sent_e = send(blocks_of(expand_grads), 1)
    mixer_out = sum(dot(a, w) for a, w in zip(activated_all, reduce_all))
    branch = attn_out + mixer_out
    layer_rows = (rows + router * branch).astype(BF16)
    router_grad = jnp.sum(cot * branch, axis=1, keepdims=True)
    layer_rows, router_grad, back_all, part_e, part_r = hold(
        (layer_rows, router_grad, back_all, merge(sent_e), merge_cross(sent_r))
    )
    sent_r = send(part_r, 2)
    sent_e = cross(part_e)
    two_grad = sum(dot(g, w, NT) for g, w in zip(back_all, expand_all))
    hidden_hat = hidden * scale_second
    weighted_two = two_grad * gain_two
    gain_two_part = jnp.sum(two_grad * hidden_hat, axis=0)
    stat_two = jnp.mean(weighted_two * hidden_hat, axis=1, keepdims=True)
    hidden_grad = scale_second * (weighted_two - hidden_hat * stat_two)
    branch_grad = (router * cot + hidden_grad).astype(BF16)
    branch_parts = branch_grad.reshape(own_rows, parts, width)
    output_grads = [
        jnp.einsum("re,rcd->ced", a, branch_parts, preferred_element_type=F32)
        .astype(BF16)
        .reshape(full, width)
        for a in attended_all
    ]
    back_heads = [dot(branch_grad, w, NT, BF16) for w in output_all]
    back_heads, output_grads, part_r = hold((back_heads, output_grads, merge(sent_r)))
    sent_r = send(part_r, 4)
    sent_o = send(blocks_of(output_grads), 1)

    def heads_back(k):
        return attention(attend_back_body, masks, cap, qkv_all[k], back_heads[k])

    def weight_grad(back):
        grad = jnp.einsum("rd,cre->cde", normed, back, preferred_element_type=F32)
        return grad.astype(BF16).reshape(3 * full, -1)

    back_far = [heads_back(k) for k in range(1, parts)]
    back_far, part_r, part_e, part_o, layer_rows = hold(
        (back_far, merge(sent_r), merge_cross(sent_e), merge(sent_o), layer_rows)
    )
    sent_e = send(part_e, 2)
    sent_o = cross(part_o)
    layer_moved = to_features(layer_rows)
    sum_r = finish(part_r, 8)
    grads_far = [weight_grad(g) for g in back_far]
    grads_far, sum_r, qkv_all = hold((grads_far, sum_r, qkv_all))
    grad_reduce = lax.all_gather(sum_r, "dp", axis=0, tiled=True)
    sent_p = send(blocks_of(grads_far), 1)
    back_own = heads_back(0)
    back_own, part_e, far_p, part_o = hold(
        (back_own, merge(sent_e), merge(sent_p), merge_cross(sent_o))
    )
    sent_e = send(part_e, 4)
    sent_o = send(part_o, 2)
    moved_p = [shift_plain(g, k + 1) for k, g in enumerate(far_p)]
    grad_own = weight_grad(back_own)
    project_back = [back_own] + back_far
    grad_own, project_back, part_e, part_o = hold(
        (grad_own, project_back, merge(sent_e), merge(sent_o))
    )
    sent_o = send(part_o, 4)
    sum_e = finish(part_e, 8)
    own_p = merge(send(blocks_of([grad_own]), 1))
    normed_grad = sum(
        dot(g[c], w[c], NT) for g, w in zip(project_back, project_all) for c in range(3)
    )
    normed_grad, sum_e, part_o = hold((normed_grad, sum_e, merge(sent_o)))
    grad_expand = lax.all_gather(sum_e, "dp", axis=0, tiled=True)
    rows_hat = rows * scale_first
    weighted_one = normed_grad * gain_one
    gain_one_part = jnp.sum(normed_grad * rows_hat, axis=0)
    stat_one = jnp.mean(weighted_one * rows_hat, axis=1, keepdims=True)
    first_grad = scale_first * (weighted_one - rows_hat * stat_one)
    rows_grad = cot + hidden_grad + first_grad + router_grad * router_row
    router_part = jnp.sum(router_grad * rows, axis=0)
    small = jnp.stack([gain_one_part, gain_two_part, router_part])
    rows_grad, part_p, small, layer_moved = hold(
        (rows_grad.astype(BF16), merge_cross((own_p, moved_p)), small, layer_moved)
    )
    sent_p = send(part_p, 2)
    rows_moved = to_features(rows_grad)
    sum_o = finish(part_o, 8)
    bit = 1
    while bit < copies:
        small = small + flip_plain(small, bit)
        bit *= 2
    total = small
    for k in range(1, parts):
        total = total + shift_plain(small, k)
    small = lax.dynamic_slice_in_dim(total, here * width, width, 1)
    layer_out = scatter_rows(layer_in, layer_moved, route_index)
    layer_out, part_p, rows_moved, sum_o = hold((layer_out, merge(sent_p), rows_moved, sum_o))
    sent_p = send(part_p, 4)
    input_grad = scatter_rows(out_grad, rows_moved, route_index)
    sum_p = finish(merge(sent_p), 8)
    lead = sum_p.shape[0]
    both = jnp.concatenate([sum_p, sum_o], axis=0)
    both, grad_reduce, grad_expand = hold((both, grad_reduce, grad_expand))
    both = lax.all_gather(both, "dp", axis=0)
    grad_project = both[:, :lead].astype(F32).reshape(3, full, width)
    output_sum = both[:, lead:].reshape(parts, width, width).transpose(1, 0, 2)
    output_sum = output_sum.reshape(width, full)
    grad_reduce = grad_reduce.astype(F32)
    grad_expand = grad_expand.astype(F32)
    output_sum = output_sum.astype(F32)
    return (
        layer_out,
        input_grad,
        grad_project,
        output_sum,
        grad_expand,
        grad_reduce,
        small[0],
        small[1],
        small[2],
    )


def labelled(sizes, *args):
    return shards(sizes, *args)


def solution(mesh):
    return jax.shard_map(
        partial(labelled, (mesh.shape["dp"], mesh.shape["tensor"])),
        mesh=mesh,
        in_specs=(
            P("dp", "tensor"),
            P("dp", "tensor"),
            P("dp", None),
            P("dp"),
            P(None, None, "tensor"),
            P("tensor", None),
            P(None, "tensor"),
            P("tensor", None),
            P(),
            P(),
            P(),
        ),
        out_specs=(
            P("dp", "tensor"),
            P("dp", "tensor"),
            P(None, None, "tensor"),
            P("tensor", None),
            P(None, "tensor"),
            P("tensor", None),
            P("tensor"),
            P("tensor"),
            P("tensor"),
        ),
        check_vma=False,
    )
```
